512 devices in a mesh: seq: 32 (over y, z_lo, core), tok: 16 (over z_hi, x).
Axes of the slice: x: 4, y: 4, z: 16 (z_hi: 4, z_lo: 4; z = z_hi * 4 + z_lo), core: 2. Of those that a mesh axis runs over, the one named last changes fastest.
Arguments:
- entering: bfloat16 [32, 512, 3, 512], P('seq', 'tok'), may hold values from -0.9059806 to 0.9059806, as said below
- fresh: bfloat16 [512, 3, 512], P('tok'), may hold values from -0.9059806 to 0.9059806, as said below
- qkv_first: bfloat16 [32, 8192, 3, 512], P('seq', 'tok'), may hold values from -6 to 6
- qkv_second: bfloat16 [32, 8192, 3, 512], P('seq', 'tok'), may hold values from -6 to 6
- rates_first: float32 [32, 8192], P('seq', 'tok'), may hold values from 5.5242715e-05 to 0.0005524272
- rates_second: float32 [32, 8192], P('seq', 'tok'), may hold values from 5.5242715e-05 to 0.0005524272
Outputs:
- out_first: bfloat16 [32, 8192, 512], P('seq', 'tok')
- out_second: bfloat16 [32, 8192, 512], P('seq', 'tok')
- leaving: bfloat16 [32, 512, 3, 512], P('seq', 'tok')
The draws below stay inside these ranges and needn't reach their ends.
Inputs may be any that keep to these rules, and one draw needn't show every extreme that they name: `entering`: fast weights of a scale near 512 ** -0.5. `fresh`: fast weights of a scale near 512 ** -0.5.
All inputs are finite; a program needn't handle non-finite values.
Results may differ from the reference program's by a relative error of at most 0.02.
Values may be sent and summed in bfloat16 or wider, within the bound.
No kernel may reach another device: no remote copies, remote signals or barrier semaphores. Data moves between devices by JAX's collectives and lax.ppermute only.
A program may use at most 64 MiB of HBM per device.

```python
import math
import jax
import jax.numpy as jnp
from jax import lax

D = 512
FF = 512
TOK_DEV = 512
SPAN = 8192
N_SEQ = 32
N_TOK = 16


def weight_block(key, leading):
    key_noise, key_rows, key_cols = jax.random.split(key, 3)
    shape = leading + (FF, 3, D)
    normal_part = jnp.clip(jax.random.normal(key_noise, shape, jnp.float32), -4.0, 4.0)
    low = math.log(0.32)
    high = math.log(3.2)
    row_scale = jnp.exp(jax.random.uniform(key_rows, leading + (FF, 3, 1), jnp.float32, low, high))
    col_scale = jnp.exp(jax.random.uniform(key_cols, leading + (1, 3, D), jnp.float32, low, high))
    return (normal_part * row_scale * col_scale * (0.5 / math.sqrt(D))).astype(jnp.bfloat16)


def draw_entering(key, part):
    return weight_block(jax.random.fold_in(key, 11), (N_SEQ,))


def draw_fresh(key, part):
    return weight_block(jax.random.fold_in(key, 12), ())


def steps_of(key, extent, cuts, smallest, largest):
    loudness = 1.0
    for position, parts in cuts:
        steps = jax.random.uniform(jax.random.fold_in(jax.random.fold_in(key, 6), position), (parts,), jnp.float32, smallest / len(cuts), largest / len(cuts))
        loudness = loudness * jnp.repeat(jnp.exp(steps), extent[position] // parts).reshape((-1,) + (1,) * (len(extent) - 1 - position))
    return loudness


def centred(stream_key, extent, scale, reach, shards=(), held_as=jnp.bfloat16):
    result = jax.random.normal(stream_key, extent, jnp.float32) * scale
    if len(shards) > 0:
        result = steps_of(stream_key, extent, shards, -0.22, 0.18) * result
    return jnp.clip(result, min=-reach, max=reach).astype(held_as)


def setup_inputs(seed: int = 0) -> dict:
    splits = jax.random.split(jax.random.key(seed), 7)
    entering = draw_entering(jax.random.fold_in(splits[6], 71), 0)
    fresh = draw_fresh(jax.random.fold_in(splits[6], 71), 0)
    qkv_first = centred(splits[2], (N_SEQ, SPAN, 3, D), 1.0, 6.0, ((0, 32), (1, 16)))
    qkv_second = centred(splits[3], (N_SEQ, SPAN, 3, D), 1.0, 6.0, ((0, 32), (1, 16)))
    rates_first = jnp.clip(jnp.exp(math.log(0.0005524272) - 2.3025852 * jax.random.uniform(splits[4], (N_SEQ, SPAN), jnp.float32) ** steps_of(splits[4], (N_SEQ, SPAN), ((0, 32), (1, 16)), -0.2, 0.2)), 5.5242715461645275e-05, 0.0005524272)
    rates_second = jnp.clip(jnp.exp(math.log(0.0005524272) - 2.3025852 * jax.random.uniform(splits[5], (N_SEQ, SPAN), jnp.float32) ** steps_of(splits[5], (N_SEQ, SPAN), ((0, 32), (1, 16)), -0.2, 0.2)), 5.5242715461645275e-05, 0.0005524272)
    return {"entering": entering, "fresh": fresh, "qkv_first": qkv_first, "qkv_second": qkv_second, "rates_first": rates_first, "rates_second": rates_second}


def forward_rows(weights, inputs):
    pre_gate = jnp.dot(inputs, weights[:, 0, :].T, preferred_element_type=jnp.float32)
    pre_up = jnp.dot(inputs, weights[:, 1, :].T, preferred_element_type=jnp.float32)
    return (pre_gate, pre_up)

def renormed(weights, gradient):
    old_values = weights.astype(jnp.float32)
    stepped = old_values - gradient
    old_norm = jnp.sqrt(lax.optimization_barrier(jnp.sum(old_values * old_values, axis=-1, keepdims=True)))
    new_norm = jnp.sqrt(lax.optimization_barrier(jnp.sum(stepped * stepped, axis=-1, keepdims=True)) + 1e-06)
    return (stepped * (old_norm / new_norm)).astype(jnp.bfloat16)

def fast_tick(weights, tick_data, token_rates):
    queries = tick_data[:, 0, :]
    key_rows = tick_data[:, 1, :]
    value_rows = tick_data[:, 2, :]
    gate_q, up_q = forward_rows(weights, queries)
    hidden_q = (jax.nn.silu(gate_q) * up_q).astype(jnp.bfloat16)
    output = jnp.dot(hidden_q, weights[:, 2, :], preferred_element_type=jnp.float32).astype(jnp.bfloat16)
    gate_k, up_k = forward_rows(weights, key_rows)
    hidden_k = (jax.nn.silu(gate_k) * up_k).astype(jnp.bfloat16)
    scaled = (-token_rates[:, None] * value_rows.astype(jnp.float32)).astype(jnp.bfloat16)
    d_hidden = jnp.dot(scaled, weights[:, 2, :].T, preferred_element_type=jnp.float32)
    sigmoid_gate = jax.nn.sigmoid(gate_k)
    d_gate = (d_hidden * up_k * sigmoid_gate * (1.0 + gate_k * (1.0 - sigmoid_gate))).astype(jnp.bfloat16)
    d_up = (d_hidden * jax.nn.silu(gate_k)).astype(jnp.bfloat16)
    width = key_rows.shape[1]
    hidden_units = weights.shape[0]

    def blocks(array):
        return array.reshape(N_TOK, TOK_DEV, array.shape[1])

    def add_partial(running, pieces):
        gate_piece, up_piece, hidden_piece, key_piece, scaled_piece = pieces
        partial_value = jnp.stack([jnp.dot(gate_piece.T, key_piece, preferred_element_type=jnp.float32), jnp.dot(up_piece.T, key_piece, preferred_element_type=jnp.float32), jnp.dot(hidden_piece.T, scaled_piece, preferred_element_type=jnp.float32)], axis=1)
        rounded = lax.optimization_barrier(partial_value.astype(jnp.bfloat16))
        return (running + rounded.astype(jnp.float32), None)
    start = jnp.zeros((hidden_units, 3, width), jnp.float32)
    gradient, _ = lax.scan(add_partial, start, (blocks(d_gate), blocks(d_up), blocks(hidden_k), blocks(key_rows), blocks(scaled)))
    return (output, renormed(weights, gradient))

def group_tick(inputs):
    return fast_tick(inputs[0], inputs[1], inputs[2])

def reference(entering, fresh, qkv_first, qkv_second, rates_first, rates_second):
    out_first, updated = lax.map(group_tick, (entering, qkv_first, rates_first))
    passed = jnp.concatenate([fresh[None], updated[:-1]], axis=0)
    out_second, leaving = lax.map(group_tick, (passed, qkv_second, rates_second))
    return (out_first, out_second, leaving)
```

```python
import jax
import jax.numpy as jnp
from jax import lax
from jax.sharding import PartitionSpec as P

SIDE = 4


def far_groups(size):
    return [[near + SIDE * far for far in range(size // SIDE)] for near in range(SIDE)]


def near_groups(size):
    return [[near + SIDE * far for near in range(SIDE)] for far in range(size // SIDE)]


def gathered(rows, groups):
    return lax.all_gather(rows, "tok", axis=0, axis_index_groups=groups)


def exchanged(blocks, groups):
    return lax.all_to_all(blocks, "tok", 0, 0, axis_index_groups=groups, tiled=True)


def summed(blocks):
    return jnp.sum(blocks.astype(jnp.float32), axis=0)


def renormed(weights, gradient):
    old_values = weights.astype(jnp.float32)
    stepped = old_values - gradient
    old_norm = jnp.sqrt(jnp.sum(old_values * old_values, axis=-1, keepdims=True))
    new_norm = jnp.sqrt(jnp.sum(stepped * stepped, axis=-1, keepdims=True) + 1e-06)
    return (stepped * (old_norm / new_norm)).astype(jnp.bfloat16)


def widened(rows):
    size = lax.axis_size("tok")
    column = gathered(rows, far_groups(size))
    half = column.shape[2] // 2
    flat = column.reshape(column.shape[0], -1, column.shape[-1])
    middle = flat.shape[1] // 2
    first = gathered(flat[:, :middle], near_groups(size))
    second = gathered(flat[:, middle:], near_groups(size))
    return jnp.concatenate([first, second], axis=2).reshape(
        (SIDE,) + column.shape
    )


def fast_tick(own_rows, tick_data, token_rates):
    size = lax.axis_size("tok")
    full = widened(own_rows)
    width = full.shape[-1]
    gate_rows = full[:, :, 0].reshape(-1, width)
    up_rows = full[:, :, 1].reshape(-1, width)
    down_rows = full[:, :, 2].reshape(-1, width)
    queries, key_rows, value_rows = tick_data
    token_count = queries.shape[0]
    contract = (((1,), (1,)), ((), ()))
    across = (((0,), (0,)), ((), ()))
    stacked = jnp.concatenate([queries, key_rows], axis=0)
    pre_gate = lax.dot_general(stacked, gate_rows, contract, preferred_element_type=jnp.float32)
    pre_up = lax.dot_general(stacked, up_rows, contract, preferred_element_type=jnp.float32)
    hidden = (jax.nn.silu(pre_gate) * pre_up).astype(jnp.bfloat16)
    output = jnp.dot(
        hidden[:token_count], down_rows, preferred_element_type=jnp.float32
    ).astype(jnp.bfloat16)
    hidden_k = hidden[token_count:]
    gate_k = pre_gate[token_count:]
    up_k = pre_up[token_count:]
    scaled = (-token_rates[:, None] * value_rows.astype(jnp.float32)).astype(jnp.bfloat16)
    d_hidden = lax.dot_general(scaled, down_rows, contract, preferred_element_type=jnp.float32)
    sigmoid_gate = jax.nn.sigmoid(gate_k)
    d_gate = (d_hidden * up_k * sigmoid_gate * (1.0 + gate_k * (1.0 - sigmoid_gate))).astype(
        jnp.bfloat16
    )
    d_up = (d_hidden * jax.nn.silu(gate_k)).astype(jnp.bfloat16)
    block = full.shape[:2] + full.shape[3:]
    partial = jnp.stack(
        [
            lax.dot_general(left, right, across, preferred_element_type=jnp.float32)
            .astype(jnp.bfloat16)
            .reshape(block)
            for left, right in ((d_gate, key_rows), (d_up, key_rows), (hidden_k, scaled))
        ],
        axis=2,
    )
    column = summed(exchanged(partial, near_groups(size))).astype(jnp.bfloat16)
    gradient = summed(exchanged(column, far_groups(size)))
    return output, renormed(own_rows, gradient)


def on_device(entering, fresh, qkv_first, qkv_second, rates_first, rates_second):
    groups = lax.axis_size("seq")
    own_rows = jnp.swapaxes(entering[0], 0, 1)
    fresh_rows = jnp.swapaxes(fresh, 0, 1)
    first_data = tuple(qkv_first[0][:, i, :] for i in range(3))
    second_data = tuple(qkv_second[0][:, i, :] for i in range(3))
    out_first, new_rows = fast_tick(own_rows, first_data, rates_first[0])
    last_group = lax.axis_index("seq") == groups - 1
    handed = jnp.where(last_group, fresh_rows, new_rows)
    second_rows = lax.ppermute(handed, "seq", [(i, (i + 1) % groups) for i in range(groups)])
    out_second, leaving_rows = fast_tick(second_rows, second_data, rates_second[0])
    leaving = jnp.swapaxes(leaving_rows, 0, 1)
    return (out_first[None], out_second[None], leaving[None])


def solution(mesh):
    placed = (
        P("seq", "tok", None, None),
        P("tok", None, None),
        P("seq", "tok", None, None),
        P("seq", "tok", None, None),
        P("seq", "tok"),
        P("seq", "tok"),
    )
    return jax.shard_map(
        on_device,
        mesh=mesh,
        in_specs=placed,
        out_specs=(P("seq", "tok", None), P("seq", "tok", None), P("seq", "tok", None, None)),
        check_vma=False,
    )
```

```python
import jax
import jax.numpy as jnp
from jax import lax
from jax.sharding import PartitionSpec as P

SIDE = 4


def far_groups(size):
    return [[near + SIDE * far for far in range(size // SIDE)] for near in range(SIDE)]


def exchanged(blocks, groups):
    return lax.all_to_all(blocks, "tok", 0, 0, axis_index_groups=groups, tiled=True)


def summed(blocks):
    return jnp.sum(blocks.astype(jnp.float32), axis=0)


def with_mate(block):
    size = lax.axis_size("tok")
    return lax.ppermute(block, "tok", [(i, i ^ 1) for i in range(size)])


def with_partner(block):
    size = lax.axis_size("tok")
    return lax.ppermute(block, "tok", [(i, i - i % SIDE + SIDE - 1 - i % SIDE) for i in range(size)])


def dotted(left, right, left_dim, right_dim):
    return lax.dot_general(
        left, right, (((left_dim,), (right_dim,)), ((), ())), preferred_element_type=jnp.float32
    )


def renormed(weights, gradient):
    old_values = weights.astype(jnp.float32)
    stepped = old_values - gradient
    old_norm = jnp.sqrt(jnp.sum(old_values * old_values, axis=-1, keepdims=True))
    new_norm = jnp.sqrt(jnp.sum(stepped * stepped, axis=-1, keepdims=True) + 1e-06)
    return (stepped * (old_norm / new_norm)).astype(jnp.bfloat16)


def split_rows(column):
    width = column.shape[-1]
    return tuple(column[:, part].reshape(-1, width) for part in range(3))


def output_piece(columns, queries):
    gate_rows, up_rows, down_rows = (
        jnp.concatenate(pieces) for pieces in zip(*(split_rows(column) for column in columns))
    )
    pre_gate = dotted(queries, gate_rows, 1, 1)
    pre_up = dotted(queries, up_rows, 1, 1)
    hidden = (jax.nn.silu(pre_gate) * pre_up).astype(jnp.bfloat16)
    return dotted(hidden, down_rows, 1, 0)


def partial_piece(column, key_rows, scaled):
    gate_rows, up_rows, down_rows = split_rows(column)
    pre_gate = dotted(key_rows, gate_rows, 1, 1)
    pre_up = dotted(key_rows, up_rows, 1, 1)
    hidden = (jax.nn.silu(pre_gate) * pre_up).astype(jnp.bfloat16)
    d_hidden = dotted(scaled, down_rows, 1, 1)
    sigmoid_gate = jax.nn.sigmoid(pre_gate)
    d_gate = (d_hidden * pre_up * sigmoid_gate * (1.0 + pre_gate * (1.0 - sigmoid_gate))).astype(
        jnp.bfloat16
    )
    d_up = (d_hidden * jax.nn.silu(pre_gate)).astype(jnp.bfloat16)
    block = column.shape[:1] + column.shape[2:]
    return jnp.stack(
        [
            dotted(left, right, 0, 0).reshape(block)
            for left, right in ((d_gate, key_rows), (d_up, key_rows), (hidden, scaled))
        ],
        axis=1,
    )


def tick_inputs(qkv, rates):
    queries, key_rows, value_rows = (qkv[:, i, :] for i in range(3))
    scaled = (-rates[:, None] * value_rows.astype(jnp.float32)).astype(jnp.bfloat16)
    pairs = jnp.stack([key_rows, scaled])
    mate_pairs = with_mate(pairs)
    mate_queries = with_mate(queries)
    key_rows, scaled = jnp.concatenate([pairs, mate_pairs], axis=1)
    return queries, mate_queries, key_rows, scaled


def finished(own_output, returned):
    return (own_output + returned.astype(jnp.float32)).astype(jnp.bfloat16)


def fast_tick(own_rows, inputs, pending=()):
    size = lax.axis_size("tok")
    own_queries, mate_queries, key_rows, scaled = inputs
    own_column = lax.all_gather(own_rows, "tok", axis=0, axis_index_groups=far_groups(size))
    partner_column = with_partner(own_column)
    own_column, *pending = lax.optimization_barrier((own_column, *pending))
    earlier = finished(*pending) if pending else None
    partner_column, earlier = lax.optimization_barrier((partner_column, earlier))
    own_partial = partial_piece(own_column, key_rows, scaled)
    partner_partial = partial_piece(partner_column, key_rows, scaled).astype(jnp.bfloat16)
    reduced = with_partner(partner_partial)
    column_sum = own_partial + reduced.astype(jnp.float32)
    scattered = exchanged(column_sum.astype(jnp.bfloat16), far_groups(size))
    gradient = summed(scattered)
    columns = (own_column, partner_column)
    mate_output = output_piece(columns, mate_queries).astype(jnp.bfloat16)
    returned = with_mate(mate_output)
    pending = (output_piece(columns, own_queries), returned)
    return pending, renormed(own_rows, gradient), earlier


def both_ticks(entering, fresh, qkv_first, qkv_second, rates_first, rates_second):
    groups = lax.axis_size("seq")
    own_rows = jnp.swapaxes(entering[0], 0, 1)
    fresh_rows = jnp.swapaxes(fresh, 0, 1)
    first_inputs = tick_inputs(qkv_first[0], rates_first[0])
    second_inputs = tick_inputs(qkv_second[0], rates_second[0])
    pending, new_rows, _ = fast_tick(own_rows, first_inputs)
    last_group = lax.axis_index("seq") == groups - 1
    handed = jnp.where(last_group, fresh_rows, new_rows)
    second_rows = lax.ppermute(handed, "seq", [(i, (i + 1) % groups) for i in range(groups)])
    last_pending, leaving_rows, out_first = fast_tick(second_rows, second_inputs, pending)
    out_second = finished(*last_pending)
    leaving = jnp.swapaxes(leaving_rows, 0, 1)
    return (out_first[None], out_second[None], leaving[None])


def solution(mesh):
    placed = (
        P("seq", "tok", None, None),
        P("tok", None, None),
        P("seq", "tok", None, None),
        P("seq", "tok", None, None),
        P("seq", "tok"),
        P("seq", "tok"),
    )
    return jax.shard_map(
        both_ticks,
        mesh=mesh,
        in_specs=placed,
        out_specs=(P("seq", "tok", None), P("seq", "tok", None), P("seq", "tok", None, None)),
        check_vma=False,
    )
```

```python
import jax
import jax.numpy as jnp
from jax import lax
from jax.experimental import pallas as pl
from jax.sharding import PartitionSpec as P

SIDE = 4


def far_groups(size):
    return [[near + SIDE * far for far in range(size // SIDE)] for near in range(SIDE)]


def exchanged(blocks, groups):
    return lax.all_to_all(blocks, "tok", 0, 0, axis_index_groups=groups, tiled=True)


def summed(blocks):
    return jnp.sum(blocks.astype(jnp.float32), axis=0)


def with_mate(block):
    size = lax.axis_size("tok")
    route = [(i, i - i % SIDE + SIDE - 1 - i % SIDE) for i in range(size)]
    return lax.ppermute(block, "tok", route)


def with_partner(block):
    size = lax.axis_size("tok")
    return lax.ppermute(block, "tok", [(i, i ^ 1) for i in range(size)])


def dotted(left, right, left_dim, right_dim):
    return lax.dot_general(
        left, right, (((left_dim,), (right_dim,)), ((), ())), preferred_element_type=jnp.float32
    )


def renormed(weights, gradient):
    old_values = weights.astype(jnp.float32)
    stepped = old_values - gradient
    old_norm = jnp.sqrt(jnp.sum(old_values * old_values, axis=-1, keepdims=True))
    new_norm = jnp.sqrt(jnp.sum(stepped * stepped, axis=-1, keepdims=True) + 1e-06)
    return (stepped * (old_norm / new_norm)).astype(jnp.bfloat16)


def unit_rows(column_ref, part):
    rows = column_ref[:, part]
    return rows.reshape(-1, rows.shape[-1])


def plane_spec(index, array):
    return pl.BlockSpec((1,) + array.shape[1:], lambda _, index=index: (index, 0, 0))


def whole_spec(array):
    rank = len(array.shape)
    return pl.BlockSpec(array.shape, lambda _: (0,) * rank)


def scaled_rows(values, rates):
    tokens = rates.shape[-1]
    column = jnp.broadcast_to(rates, (128, tokens)).T[:, :1]
    return (-column * values.astype(jnp.float32)).astype(jnp.bfloat16)


def tokens_kernel(*refs):
    *source_refs, tokens_ref = refs
    count = source_refs[0].shape[1]
    for place in range(len(source_refs) // 3):
        keys_ref, values_ref, rates_ref = source_refs[3 * place : 3 * place + 3]
        here = pl.ds(place * count, count)
        tokens_ref[0, here] = keys_ref[0]
        tokens_ref[1, here] = scaled_rows(values_ref[0], rates_ref[...])


def token_pairs(*sources):
    arrays, specs = [], []
    for planes, rates in sources:
        arrays += [planes, planes, rates]
        specs += [plane_spec(1, planes), plane_spec(2, planes), whole_spec(rates)]
    count, width = sources[0][0].shape[1:]
    shape = jax.ShapeDtypeStruct((2, len(sources) * count, width), jnp.bfloat16)
    return pl.pallas_call(
        tokens_kernel,
        out_shape=shape,
        grid=(1,),
        in_specs=specs,
        out_specs=whole_spec(shape),
    )(*arrays)


def split_rows(column):
    width = column.shape[-1]
    return tuple(column[:, part].reshape(-1, width) for part in range(3))


def partial_piece(column, key_rows, scaled):
    gate_rows, up_rows, down_rows = split_rows(column)
    pre_gate = dotted(key_rows, gate_rows, 1, 1)
    pre_up = dotted(key_rows, up_rows, 1, 1)
    hidden = (jax.nn.silu(pre_gate) * pre_up).astype(jnp.bfloat16)
    d_hidden = dotted(scaled, down_rows, 1, 1)
    sigmoid_gate = jax.nn.sigmoid(pre_gate)
    d_gate = (d_hidden * pre_up * sigmoid_gate * (1.0 + pre_gate * (1.0 - sigmoid_gate))).astype(
        jnp.bfloat16
    )
    d_up = (d_hidden * jax.nn.silu(pre_gate)).astype(jnp.bfloat16)
    block = column.shape[:1] + column.shape[2:]
    return jnp.stack(
        [
            dotted(left, right, 0, 0).reshape(block)
            for left, right in ((d_gate, key_rows), (d_up, key_rows), (hidden, scaled))
        ],
        axis=1,
    )


def output_kernel(first_ref, second_ref, queries_ref, *refs):
    *returned_refs, output_ref = refs
    queries = queries_ref[0]
    total = 0.0
    for column_ref in (first_ref, second_ref):
        gate_rows, up_rows, down_rows = (unit_rows(column_ref, part) for part in range(3))
        pre_gate = dotted(queries, gate_rows, 1, 1)
        pre_up = dotted(queries, up_rows, 1, 1)
        hidden = (pre_gate * jax.nn.sigmoid(pre_gate) * pre_up).astype(jnp.bfloat16)
        total = total + dotted(hidden, down_rows, 1, 0)
    for returned_ref in returned_refs:
        total = total + returned_ref[...].astype(jnp.float32)
    output_ref[...] = total.astype(jnp.bfloat16)


def output_piece(columns, planes, *returned):
    shape = jax.ShapeDtypeStruct(planes.shape[1:], jnp.bfloat16)
    return pl.pallas_call(
        output_kernel,
        out_shape=shape,
        in_specs=[
            *(whole_spec(column) for column in columns),
            plane_spec(0, planes),
            *(whole_spec(array) for array in returned),
        ],
        grid=(1,),
        out_specs=whole_spec(shape),
    )(*columns, planes, *returned)


def scattered_of(column_sum):
    return exchanged(column_sum.astype(jnp.bfloat16), far_groups(lax.axis_size("tok")))


def gathered_column(rows):
    groups = far_groups(lax.axis_size("tok"))
    return lax.all_gather(rows, "tok", axis=0, axis_index_groups=groups)


def column_pair(own_rows):
    own_column = gathered_column(own_rows)
    return own_column, with_partner(own_column)


def column_total(own_column, partner_column, tokens):
    own_partial = partial_piece(own_column, *tokens)
    own_partial, partner_column = lax.optimization_barrier((own_partial, partner_column))
    partner_partial = partial_piece(partner_column, *tokens).astype(jnp.bfloat16)
    reduced = with_partner(partner_partial)
    return own_partial + reduced.astype(jnp.float32)


def both_ticks(entering, fresh, qkv_first, qkv_second, rates_first, rates_second):
    groups = lax.axis_size("seq")
    own_rows = jnp.swapaxes(entering[0], 0, 1)
    fresh_rows = jnp.swapaxes(fresh, 0, 1)
    first_planes = jnp.swapaxes(qkv_first[0], 0, 1)
    second_planes = jnp.swapaxes(qkv_second[0], 0, 1)
    first_pairs = token_pairs((first_planes, rates_first))
    first_mate = with_mate(first_pairs)
    first_mate_queries = with_mate(first_planes[:1])
    second_pairs = token_pairs((second_planes, rates_second))
    second_mate = with_mate(second_pairs)
    second_mate_queries = with_mate(second_planes[:1])

    first_columns = column_pair(own_rows)
    tokens = jnp.concatenate([first_pairs, first_mate], axis=1)
    column_sum = column_total(*first_columns, tokens)
    scattered = scattered_of(column_sum)
    mate_output = output_piece(first_columns, first_mate_queries)
    returned = with_mate(mate_output)
    new_rows = renormed(own_rows, summed(scattered))

    last_group = lax.axis_index("seq") == groups - 1
    handed = jnp.where(last_group, fresh_rows, new_rows)
    second_rows = lax.ppermute(handed, "seq", [(i, (i + 1) % groups) for i in range(groups)])
    tokens = jnp.concatenate([second_pairs, second_mate], axis=1)
    second_rows, tokens = lax.optimization_barrier((second_rows, tokens))
    own_column, partner_column = column_pair(second_rows)
    own_column, returned = lax.optimization_barrier((own_column, returned))
    out_first = output_piece(first_columns, first_planes, returned)
    column_sum = column_total(own_column, partner_column, tokens)
    second_columns = (own_column, partner_column)
    mate_output = output_piece(second_columns, second_mate_queries)
    column_sum, mate_output = lax.optimization_barrier((column_sum, mate_output))
    scattered = scattered_of(column_sum)
    returned = with_mate(mate_output)
    out_second = output_piece(second_columns, second_planes, returned)
    leaving = jnp.swapaxes(renormed(second_rows, summed(scattered)), 0, 1)
    return (out_first[None], out_second[None], leaving[None])


def solution(mesh):
    placed = (
        P("seq", "tok", None, None),
        P("tok", None, None),
        P("seq", "tok", None, None),
        P("seq", "tok", None, None),
        P("seq", "tok"),
        P("seq", "tok"),
    )
    return jax.shard_map(
        both_ticks,
        mesh=mesh,
        in_specs=placed,
        out_specs=(P("seq", "tok", None), P("seq", "tok", None), P("seq", "tok", None, None)),
        check_vma=False,
    )
```
